32 devices in a mesh: bin: 4 (over z), tile: 8 (over y, x, core).
Axes of the slice: x: 2, y: 2, z: 4, core: 2. Of those that a mesh axis runs over, the one named last changes fastest.
Arguments:
- numbers: float32 [2, 40, 16, 128, 128], P(None, 'bin', 'tile'), may hold values from 0.05 to 1
- adjoint: float32 [40, 16, 128, 128], P('bin', 'tile'), may hold values from -6 to 6
- courant_x: float32 [16, 128, 128], P('tile'), may hold values from 0.02 to 0.3
- courant_y: float32 [16, 128, 128], P('tile'), may hold values from 0.02 to 0.3
- column_mask: int32 [16, 128], replicated, may hold values from 0 to 1, as said below
- level_count: int32 [16, 128], replicated, may hold values from 1 to 128
- settling: float32 [40, 128], replicated, may hold values from 0.02 to 0.5
- kernel_scale: float32 [128], replicated, may hold values from 1e-05 to 0.0001
Outputs:
- adjoint_out: float32 [40, 16, 128, 128], P('bin', 'tile')
The draws below stay inside these ranges and needn't reach their ends.
Inputs may be any that keep to these rules, and one draw needn't show every extreme that they name: `column_mask`: 0 or 1 for each column.
All inputs are finite; a program needn't handle non-finite values.
Results may differ from the reference program's by a relative error of at most 0.0001.
Values sent between devices are 32-bit elements; how exact they have to be, the bound alone decides.
No kernel may reach another device: no remote copies, remote signals or barrier semaphores. Data moves between devices by JAX's collectives and lax.ppermute only.
A program may use at most 64 MiB of HBM per device.

```python
import math
import jax
import jax.numpy as jnp
import numpy as np
from jax import lax

NB = 40
LEV = 128
NY = 128
STEPS = 2
NX = 16


def draw_column_mask(key, part):
    plume_key, level_key = jax.random.split(jax.random.fold_in(key, 17))
    plume_start = jax.random.randint(plume_key, (), 0, NX)
    row_index = jnp.arange(NX)
    inside = (row_index - plume_start) % NX < NX // 4
    rolled = jax.random.randint(level_key, (NX, NY), 0, 100)
    threshold = jnp.where(inside, 90, 20)
    return (rolled < threshold[:, None]).astype(jnp.int32)


def set_ends(entries, key, least, top_value):
    longest = entries.shape.index(max(entries.shape))
    spots = []
    for shift in (0, 1):
        where = [jax.random.randint(jax.random.fold_in(key, axis), (), 0, length) for axis, length in enumerate(entries.shape)]
        where[longest] = (where[longest] + shift) % entries.shape[longest]
        spots.append(tuple(where))
    return entries.at[spots[0]].set(least).at[spots[1]].set(top_value)


def steps_of(key, extent, cuts, least, largest):
    def one(axis_at, shards_of):
        draws = jax.random.uniform(jax.random.fold_in(jax.random.fold_in(key, 6), axis_at), (shards_of,), jnp.float32, least / len(cuts), largest / len(cuts))
        return jnp.repeat(jnp.exp(draws), extent[axis_at] // shards_of).reshape((-1,) + (1,) * (len(extent) - axis_at - 1))

    level = one(*cuts[0])
    for cut in cuts[1:]:
        level = level * one(*cut)
    return level


def bell_draw(key, shape, deviation, reach, cuts=(), held_as=jnp.bfloat16):
    drawn = jax.random.normal(key, shape, jnp.float32) * deviation
    if len(cuts) > 0:
        drawn = steps_of(key, shape, cuts, -0.22, 0.18) * drawn
    return jnp.clip(drawn, min=-reach, max=reach).astype(held_as)


def setup_inputs(seed: int = 0) -> dict:
    splits = jax.random.split(jax.random.key(seed), 9)
    numbers = jnp.clip(jnp.exp(math.log(1.0) - 2.9957323 * jax.random.uniform(splits[0], (STEPS, NB, NX, NY, LEV), jnp.float32) ** steps_of(splits[0], (STEPS, NB, NX, NY, LEV), ((1, 4), (2, 8)), -0.2, 0.2)), 0.05, 1.0)
    adjoint = bell_draw(splits[1], (NB, NX, NY, LEV), 1.0, 6.0, ((0, 4), (1, 8)), jnp.float32)
    courant_x = jnp.clip(0.02 + 0.28 * jax.random.uniform(splits[2], (NX, NY, LEV), jnp.float32) ** steps_of(splits[2], (NX, NY, LEV), ((0, 8),), -0.2, 0.2), 0.02, 0.3)
    courant_y = jnp.clip(0.02 + 0.28 * jax.random.uniform(splits[3], (NX, NY, LEV), jnp.float32) ** steps_of(splits[3], (NX, NY, LEV), ((0, 8),), -0.2, 0.2), 0.02, 0.3)
    column_mask = draw_column_mask(jax.random.fold_in(splits[8], 71), 0)
    level_count = set_ends(jax.random.randint(splits[5], (NX, NY), 1, LEV + 1), jax.random.fold_in(splits[5], 1), 1, LEV).astype(jnp.int32)
    settling = jnp.clip(jax.random.uniform(splits[6], (NB, LEV), jnp.float32, 0.02, 0.5), 0.02, 0.5)
    kernel_scale = jnp.clip(jnp.exp(jax.random.uniform(splits[7], (LEV,), jnp.float32, math.log(9.999999747378752e-06), math.log(0.0001))), 9.999999747378752e-06, 0.0001)
    return {"numbers": numbers, "adjoint": adjoint, "courant_x": courant_x, "courant_y": courant_y, "column_mask": column_mask, "level_count": level_count, "settling": settling, "kernel_scale": kernel_scale}


DIFFUSION = 0.08


def pair_tables(bin_count):
    smaller_bins, larger_bins = np.triu_indices(bin_count)
    pair_count = smaller_bins.shape[0]
    pair_slots = ((pair_count + 127) // 128) * 128
    redistribute = np.zeros((bin_count, pair_slots))
    incidence = np.zeros((bin_count, 2 * pair_slots))
    kernel = np.zeros((pair_slots,))
    for pair_index in range(pair_count):
        smaller = int(smaller_bins[pair_index])
        larger = int(larger_bins[pair_index])
        weight = 0.5 if smaller == larger else 1.0
        fraction = 2.0 ** (smaller - larger)
        redistribute[smaller, pair_index] -= weight
        redistribute[larger, pair_index] -= weight
        if larger < bin_count - 1:
            redistribute[larger, pair_index] += weight * (1.0 - fraction)
            redistribute[larger + 1, pair_index] += weight * fraction
        else:
            redistribute[larger, pair_index] += weight
        incidence[smaller, pair_index] = 1.0
        incidence[larger, pair_slots + pair_index] = 1.0
        radius_ratio = 2.0 ** ((smaller - larger) / 3.0)
        kernel[pair_index] = 2.0 + radius_ratio + 1.0 / radius_ratio
    return (jnp.asarray(redistribute.T, jnp.float32), jnp.asarray(incidence, jnp.float32),
            jnp.asarray(incidence.T, jnp.float32), jnp.asarray(kernel, jnp.float32))


def flows(adjoint, ahead_x, behind_x, courant_x, courant_y):
    edge_y = jnp.zeros_like(adjoint[:, :, :1])
    ahead_y = jnp.concatenate([adjoint[:, :, 1:], edge_y], axis=2)
    behind_y = jnp.concatenate([edge_y, adjoint[:, :, :-1]], axis=2)
    flow_x = courant_x[None] * (ahead_x - adjoint) + DIFFUSION * (ahead_x - 2.0 * adjoint + behind_x)
    flow_y = courant_y[None] * (ahead_y - adjoint) + DIFFUSION * (ahead_y - 2.0 * adjoint + behind_y)
    return flow_x + flow_y


def box_tendency(numbers_part, adjoint_part, active_part, settling, kernel_scale, tables):
    redistribute_t, incidence, incidence_t, kernel = tables
    bins_all, col_count, levels = adjoint_part.shape
    pair_slots = kernel.shape[0]
    adjoint_flat = adjoint_part.reshape(bins_all, col_count * levels)
    numbers_flat = numbers_part.reshape(bins_all, col_count * levels)
    mixed_adjoint = jnp.dot(redistribute_t, adjoint_flat, precision=lax.Precision.HIGHEST, preferred_element_type=jnp.float32)
    pair_numbers = jnp.dot(incidence_t, numbers_flat, precision=lax.Precision.HIGHEST, preferred_element_type=jnp.float32)
    weighted = mixed_adjoint * kernel[:, None] * jnp.tile(kernel_scale, col_count)[None, :]
    stacked = jnp.concatenate([weighted * pair_numbers[pair_slots:], weighted * pair_numbers[:pair_slots]], axis=0)
    coag_gain = jnp.dot(incidence, stacked, precision=lax.Precision.HIGHEST, preferred_element_type=jnp.float32)
    coag_gain = coag_gain.reshape(bins_all, col_count, levels)
    edge_z = jnp.zeros_like(adjoint_part[:, :, :1])
    level_below = jnp.concatenate([edge_z, adjoint_part[:, :, :-1]], axis=2)
    settle = settling[:, None, :] * (level_below - adjoint_part)
    return active_part[None] * (coag_gain + settle)


def reference(numbers, adjoint, courant_x, courant_y, column_mask, level_count, settling, kernel_scale):
    tables = pair_tables(adjoint.shape[0])
    level_index = jnp.arange(kernel_scale.shape[0], dtype=jnp.int32)
    active = ((column_mask[:, :, None] == 1) & (level_index[None, None, :] < level_count[:, :, None])).astype(jnp.float32)
    result = adjoint
    for step_index in range(numbers.shape[0]):
        edge_x = jnp.zeros_like(result[:, :1])
        ahead_x = jnp.concatenate([result[:, 1:], edge_x], axis=1)
        behind_x = jnp.concatenate([edge_x, result[:, :-1]], axis=1)
        transported = flows(result, ahead_x, behind_x, courant_x, courant_y)

        def one_slab(slab):
            return box_tendency(slab[0], slab[1], slab[2], settling, kernel_scale, tables)

        slabs = (jnp.moveaxis(numbers[step_index], 1, 0), jnp.moveaxis(result, 1, 0), active)
        boxed = jnp.moveaxis(lax.map(one_slab, slabs), 0, 1)
        result = result + transported + boxed
    return result
```

```python
import functools

import jax
import jax.numpy as jnp
import numpy as np
from jax import lax
from jax.experimental import pallas as pl
from jax.experimental.pallas import tpu as pltpu
from jax.sharding import PartitionSpec as P

DIFFUSION = 0.08

WEIGHTS = (2.0, 1.0, 1.0)
FLAT = (1.0, 2.0 ** (-1.0 / 3.0), 2.0 ** (1.0 / 3.0))
STEEP = (0.5, 2.0 ** (-4.0 / 3.0), 2.0 ** (-2.0 / 3.0))

ROWS = 16


def weighted_sum(state):
    total = None
    for weight, part in zip(WEIGHTS, state):
        term = part if weight == 1.0 else weight * part
        total = term if total is None else total + term
    return total


def scaled(ratio, value):
    return value if ratio == 1.0 else ratio * value


def suffix(state, ratios, value):
    if state is None:
        return [value for _ in ratios]
    return [value + scaled(ratio, part) for ratio, part in zip(ratios, state)]


def prefix(state, ratios, value):
    if state is None:
        return [scaled(ratio, value) for ratio in ratios]
    return [scaled(ratio, part + value) for ratio, part in zip(ratios, state)]


def number_sums(numbers, write):
    down = up = None
    for value in reversed(numbers):
        down = suffix(down, FLAT, value)
    for value in numbers:
        up = prefix(up, STEEP, value)
    for field in range(3):
        write(0, field, down[field])
        write(1, field, up[field])


def adjoint_sums(numbers, adjoint, not_last, write):
    top = len(adjoint) - 1
    down = up = None
    for m in range(top, -1, -1):
        change = adjoint[m + 1] - adjoint[m] if m < top else -not_last * adjoint[m]
        down = suffix(down, STEEP, change * numbers[m])
    for m in range(top + 1):
        up = prefix(up, FLAT, adjoint[m] * numbers[m])
    for field in range(3):
        write(0, field, down[field])
        write(1, field, up[field])
    write(0, 3, adjoint[0])
    write(1, 3, adjoint[0])


def start_kernel(width, flags, numbers, adjoint, adjoint_out, numbers_out):
    bins = adjoint.shape[0]
    not_last = (flags[0] < flags[1]).astype(jnp.float32)

    def put(out, x):
        def write(slot, field, value):
            out[slot, field, x] = value

        return write

    for x in range(width):
        n = [numbers[0, k, x] for k in range(bins)]
        a = [adjoint[k, x] for k in range(bins)]
        adjoint_sums(n, a, not_last, put(adjoint_out, x))
        number_sums(n, put(numbers_out, x))


def later_kernel(width, numbers, numbers_out):
    bins = numbers.shape[1]

    for x in range(width):
        def write(slot, field, value):
            numbers_out[slot, field, x] = value

        number_sums([numbers[0, k, x] for k in range(bins)], write)


def step_kernel(width, hops, last_step, *refs):
    refs = list(refs)
    flags, numbers, adjoint, above, below, ahead, behind, cx, cy, active, settling, scale = refs[:12]
    refs = refs[12:]
    adjoint_in, refs = refs[:hops], refs[hops:]
    numbers_in, refs = refs[:hops], refs[hops:]
    if last_step:
        (out,) = refs
    else:
        numbers_next, out, sums_out = refs
    bins, _, rows, levels = adjoint.shape
    place, top_place = flags[0], flags[1]
    not_last = (place < top_place).astype(jnp.float32)
    block, blocks = pl.program_id(0), pl.num_programs(0)
    has_above = (block > 0).astype(jnp.float32)
    has_below = (block < blocks - 1).astype(jnp.float32)
    row = lax.broadcasted_iota(jnp.int32, (rows, levels), 0)
    level = lax.broadcasted_iota(jnp.int32, (rows, levels), 1)

    def arrived(parts, field, x, stage):
        value = jnp.zeros((rows, levels), jnp.float32)
        for s, part in enumerate(parts):
            value = jnp.where(stage == s + 1, part[field, x], value)
        return value

    for x in range(width):
        n = [numbers[0, k, x] for k in range(bins)]
        a = [adjoint[k, x] for k in range(bins)]
        from_above, from_below = top_place - place, place
        a_first = arrived(adjoint_in, 3, x, from_above)
        d = [a[k + 1] - a[k] for k in range(bins - 1)] + [not_last * (a_first - a[-1])]
        flat = [arrived(numbers_in, f, x, from_above) for f in range(3)]
        steep = [arrived(adjoint_in, f, x, from_above) for f in range(3)]
        part = [None] * bins
        for m in range(bins - 1, -1, -1):
            flat = suffix(flat, FLAT, n[m])
            steep = suffix(steep, STEEP, d[m] * n[m])
            part[m] = weighted_sum(steep) - a[m] * weighted_sum(flat)
        flat = [arrived(adjoint_in, f, x, from_below) for f in range(3)]
        steep = [arrived(numbers_in, f, x, from_below) for f in range(3)]
        act = active[x]
        factor = act * scale[...]
        new = []
        for m in range(bins):
            coag = part[m] + d[m] * weighted_sum(steep) - weighted_sum(flat)
            if m < bins - 1:
                flat = prefix(flat, FLAT, a[m] * n[m])
                steep = prefix(steep, STEEP, n[m])
            x_next = a_x = adjoint[m, x + 1] if x < width - 1 else ahead[m, 0]
            x_last = adjoint[m, x - 1] if x > 0 else behind[m, 0]
            above_row = above[m, x, above.shape[2] - 1 :, :] * has_above
            below_row = below[m, x, :1, :] * has_below
            y_last = jnp.where(row == 0, above_row, pltpu.roll(a[m], 1, 0))
            y_next = jnp.where(row == rows - 1, below_row, pltpu.roll(a[m], rows - 1, 0))
            z_last = jnp.where(level == 0, 0.0, pltpu.roll(a[m], 1, 1))
            moved = (
                cx[x] * (x_next - a[m])
                + cy[x] * (y_next - a[m])
                + DIFFUSION * ((x_next + x_last) + (y_next + y_last) - 4.0 * a[m])
            )
            settle = settling[m : m + 1, :] * (z_last - a[m])
            value = a[m] + moved + (factor * coag + act * settle)
            out[m, x] = value
            new.append(value)
        if not last_step:
            def write(slot, field, value):
                sums_out[slot, field, x] = value

            adjoint_sums([numbers_next[0, k, x] for k in range(bins)], new, not_last, write)


def hop_pairs(count):
    return [[(count - s, count - s - 1), (s - 1, s)] for s in range(1, count)]


def send_along(sums, decay, place, count, edge):
    got = []
    arrived = None
    for s, pairs in enumerate(hop_pairs(count), start=1):
        down = place == count - s
        slot = jnp.where(down, 0, 1)
        own = lax.dynamic_index_in_dim(sums, slot, 0, keepdims=False)
        if arrived is not None:
            ratio = lax.dynamic_index_in_dim(jnp.asarray(decay, jnp.float32), slot, 0, keepdims=False)
            own = own + ratio[:, None, None, None] * arrived
            if edge is not None:
                weights, top = edge
                factor = jnp.where(down, jnp.asarray(weights, jnp.float32), 0.0)
                own = own + factor[:, None, None, None] * (arrived[3] * top)[None]
        if count % 2 == 0:
            arrived = lax.ppermute(own, "bin", pairs)
        else:
            arrived = lax.ppermute(own, "bin", pairs[:1])
            arrived = arrived + lax.ppermute(own, "bin", pairs[1:])
        got.append(arrived)
    return got


def body(numbers, adjoint, courant_x, courant_y, column_mask, level_count, settling, kernel_scale):
    count = lax.axis_size("bin")
    tiles = lax.axis_size("tile")
    place = lax.axis_index("bin")
    tile = lax.axis_index("tile")
    bins, width, width_y, levels = adjoint.shape
    steps = numbers.shape[0]
    rows = ROWS
    blocks = width_y // rows
    halo = 8

    lam_flat = [ratio**bins for ratio in FLAT]
    lam_steep = [ratio**bins for ratio in STEEP]
    numbers_decay = np.array([lam_flat, lam_steep], np.float32)
    adjoint_decay = np.array([lam_steep + [0.0], lam_flat + [0.0]], np.float32)
    edge_weights = np.array([ratio ** (bins - 1) for ratio in STEEP] + [0.0], np.float32)

    flags = jnp.stack([place, jnp.full_like(place, count - 1)]).astype(jnp.int32)
    mask_cols = lax.dynamic_slice_in_dim(column_mask, tile * width, width, 0)
    count_cols = lax.dynamic_slice_in_dim(level_count, tile * width, width, 0)
    level_index = jnp.arange(levels, dtype=jnp.int32)
    active = ((mask_cols[:, :, None] == 1) & (level_index < count_cols[:, :, None])).astype(jnp.float32)
    own_settling = lax.dynamic_slice_in_dim(settling, place * bins, bins, 0)
    scale = kernel_scale[None, :]

    smem = pl.BlockSpec(memory_space=pltpu.SMEM)
    field = lambda n, step=None: pl.BlockSpec((n, width, rows, levels), lambda i: (0, 0, i, 0))
    pair_field = lambda n: pl.BlockSpec((2, n, width, rows, levels), lambda i: (0, 0, 0, i, 0))
    numbers_spec = lambda step: pl.BlockSpec((1, bins, width, rows, levels), lambda i: (step, 0, 0, i, 0))
    column = pl.BlockSpec((bins, 1, rows, levels), lambda i: (0, 0, i, 0))
    plane = pl.BlockSpec((width, rows, levels), lambda i: (0, i, 0))
    per = rows // halo
    above_spec = pl.BlockSpec((bins, width, halo, levels), lambda i: (0, 0, jnp.maximum(i * per - 1, 0), 0))
    below_spec = pl.BlockSpec(
        (bins, width, halo, levels), lambda i: (0, 0, jnp.minimum((i + 1) * per, blocks * per - 1), 0)
    )
    params = pltpu.CompilerParams(dimension_semantics=("arbitrary",))
    shape = lambda *dims: jax.ShapeDtypeStruct(dims, jnp.float32)

    adjoint_own, numbers_own = pl.pallas_call(
        functools.partial(start_kernel, width),
        grid=(blocks,),
        in_specs=[smem, numbers_spec(0), field(bins)],
        out_specs=[pair_field(4), pair_field(3)],
        out_shape=[shape(2, 4, width, width_y, levels), shape(2, 3, width, width_y, levels)],
        compiler_params=params,
        name="start_sums",
    )(flags, numbers, adjoint)

    def later(step):
        return pl.pallas_call(
            functools.partial(later_kernel, width),
            grid=(blocks,),
            in_specs=[numbers_spec(step)],
            out_specs=pair_field(3),
            out_shape=shape(2, 3, width, width_y, levels),
            compiler_params=params,
            name="later_sums",
        )(numbers)

    def number_chain(own):
        return send_along(own, numbers_decay, place, count, None)

    def adjoint_chain(own, step):
        return send_along(own, adjoint_decay, place, count, (edge_weights, numbers[step, bins - 1]))

    hops = count - 1
    adjoint_in = adjoint_chain(adjoint_own, 0)
    numbers_in = [number_chain(numbers_own)]
    for step in range(1, steps):
        numbers_in.append(number_chain(later(step)))

    forward = [(i, i + 1) for i in range(tiles - 1)]
    backward = [(i + 1, i) for i in range(tiles - 1)]
    for step in range(steps):
        last = step == steps - 1
        ahead = lax.ppermute(adjoint[:, :1], "tile", backward)
        behind = lax.ppermute(adjoint[:, width - 1 :], "tile", forward)
        out_specs = [field(bins)]
        out_shape = [shape(bins, width, width_y, levels)]
        extra_specs, extra = [], []
        if not last:
            out_specs.append(pair_field(4))
            out_shape.append(shape(2, 4, width, width_y, levels))
            extra_specs.append(numbers_spec(step + 1))
            extra.append(numbers)
        result = pl.pallas_call(
            functools.partial(step_kernel, width, hops, last),
            grid=(blocks,),
            in_specs=[smem, numbers_spec(step), field(bins), above_spec, below_spec, column, column]
            + [plane, plane, plane]
            + [pl.BlockSpec((bins, levels), lambda i: (0, 0)), pl.BlockSpec((1, levels), lambda i: (0, 0))]
            + [field(4)] * hops
            + [field(3)] * hops
            + extra_specs,
            out_specs=out_specs,
            out_shape=out_shape,
            compiler_params=params,
            name="step",
        )(
            flags, numbers, adjoint, adjoint, adjoint, ahead, behind, courant_x, courant_y, active,
            own_settling, scale, *adjoint_in, *numbers_in[step], *extra,
        )
        adjoint = result[0]
        if not last:
            adjoint_in = adjoint_chain(result[1], step + 1)
    return adjoint


def solution(mesh):
    return jax.shard_map(
        body,
        mesh=mesh,
        in_specs=(
            P(None, "bin", "tile", None, None),
            P("bin", "tile", None, None),
            P("tile", None, None),
            P("tile", None, None),
            P(),
            P(),
            P(),
            P(),
        ),
        out_specs=P("bin", "tile", None, None),
        check_vma=False,
    )
```
